32 devices in a mesh: rep: 4 (over x, core), shard: 4 (over z), ctx: 2 (over y).
Axes of the slice: x: 2, y: 2, z: 4, core: 2. Of those that a mesh axis runs over, the one named last changes fastest.
Arguments:
- block_input: bfloat16 [16, 256, 768], P(('rep', 'shard'), 'ctx'), may hold values from -6 to 6
- cotangent: bfloat16 [16, 256, 768], P(('rep', 'shard'), 'ctx'), may hold values from -6 to 6
- attend: float32 [2, 768, 2304], P(None, ('shard', 'ctx')), may hold values from -4 to 4
- project: float32 [2, 768, 768], P(None, ('shard', 'ctx')), may hold values from -1.25 to 1.25
- expand: float32 [2, 768, 3072], P(None, ('shard', 'ctx')), may hold values from -0.21875 to 0.21875
- contract: float32 [2, 3072, 768], P(None, ('shard', 'ctx')), may hold values from -0.109375 to 0.109375
- gains: float32 [2, 2, 768], P(None, None, ('shard', 'ctx')), may hold values from 0.5 to 1.5
- biases: float32 [2, 11, 768], P(None, None, ('shard', 'ctx')), may hold values from -3 to 3
- attend_drift: float32 [2, 768, 2304], P(None, ('shard', 'ctx')), may hold values from -112 to 112
- project_drift: float32 [2, 768, 768], P(None, ('shard', 'ctx')), may hold values from -20 to 20
- expand_drift: float32 [2, 768, 3072], P(None, ('shard', 'ctx')), may hold values from -40 to 40
- contract_drift: float32 [2, 3072, 768], P(None, ('shard', 'ctx')), may hold values from -28 to 28
- gains_drift: float32 [2, 2, 768], P(None, None, ('shard', 'ctx')), may hold values from -80 to 80
- biases_drift: float32 [2, 11, 768], P(None, None, ('shard', 'ctx')), may hold values from -112 to 112
- attend_spread: float32 [2, 768, 2304], P(None, ('shard', 'ctx')), may hold values from 204.8 to 8192
- project_spread: float32 [2, 768, 768], P(None, ('shard', 'ctx')), may hold values from 4.096 to 81.92
- expand_spread: float32 [2, 768, 3072], P(None, ('shard', 'ctx')), may hold values from 20.48 to 409.6
- contract_spread: float32 [2, 3072, 768], P(None, ('shard', 'ctx')), may hold values from 12.288 to 204.8
- gains_spread: float32 [2, 2, 768], P(None, None, ('shard', 'ctx')), may hold values from 81.92 to 1638.4
- biases_spread: float32 [2, 11, 768], P(None, None, ('shard', 'ctx')), may hold values from 204.8 to 8192
Outputs:
- block_output: float32 [16, 256, 768], P(('rep', 'shard'), 'ctx')
- input_grad: float32 [16, 256, 768], P(('rep', 'shard'), 'ctx')
- attend_grad: float32 [2, 768, 2304], P(None, ('shard', 'ctx'))
- project_grad: float32 [2, 768, 768], P(None, ('shard', 'ctx'))
- expand_grad: float32 [2, 768, 3072], P(None, ('shard', 'ctx'))
- contract_grad: float32 [2, 3072, 768], P(None, ('shard', 'ctx'))
- gains_grad: float32 [2, 2, 768], P(None, None, ('shard', 'ctx'))
- biases_grad: float32 [2, 11, 768], P(None, None, ('shard', 'ctx'))
- attend_next: float32 [2, 768, 2304], P(None, ('shard', 'ctx'))
- project_next: float32 [2, 768, 768], P(None, ('shard', 'ctx'))
- expand_next: float32 [2, 768, 3072], P(None, ('shard', 'ctx'))
- contract_next: float32 [2, 3072, 768], P(None, ('shard', 'ctx'))
- gains_next: float32 [2, 2, 768], P(None, None, ('shard', 'ctx'))
- biases_next: float32 [2, 11, 768], P(None, None, ('shard', 'ctx'))
- moment_attend: float32 [2, 768, 2304], P(None, ('shard', 'ctx'))
- moment_project: float32 [2, 768, 768], P(None, ('shard', 'ctx'))
- moment_expand: float32 [2, 768, 3072], P(None, ('shard', 'ctx'))
- moment_contract: float32 [2, 3072, 768], P(None, ('shard', 'ctx'))
- moment_gains: float32 [2, 2, 768], P(None, None, ('shard', 'ctx'))
- moment_biases: float32 [2, 11, 768], P(None, None, ('shard', 'ctx'))
- square_attend: float32 [2, 768, 2304], P(None, ('shard', 'ctx'))
- square_project: float32 [2, 768, 768], P(None, ('shard', 'ctx'))
- square_expand: float32 [2, 768, 3072], P(None, ('shard', 'ctx'))
- square_contract: float32 [2, 3072, 768], P(None, ('shard', 'ctx'))
- square_gains: float32 [2, 2, 768], P(None, None, ('shard', 'ctx'))
- square_biases: float32 [2, 11, 768], P(None, None, ('shard', 'ctx'))
The draws below stay inside these ranges and needn't reach their ends.
All inputs are finite; a program needn't handle non-finite values.
Results may differ from the reference program's by a relative error of at most 0.023.
The reference program's roundings to bfloat16 on the way count: a program that leaves them out, or rounds other values in their place, can miss the bound.
Values may be sent and summed in bfloat16 or wider, within the bound.
No kernel may reach another device: no remote copies, remote signals or barrier semaphores. Data moves between devices by JAX's collectives and lax.ppermute only.
A program may use at most 256 MiB of HBM per device.

```python
import math
import jax
import jax.numpy as jnp
from jax import lax

D = 768
HEAD = 64
ROT = 16
FF = 3072
LAYERS = 2
STEP = 3
LEN = 256
SEQS = 16


def draw_attend(key, part):
    base = jax.random.truncated_normal(key, -6.0, 6.0, (LAYERS, D, 3 * D), jnp.float32) * D ** (-0.5)
    return base


def levels(key, shape, pieces, least, top_value):
    level = 1.0
    for position, parts in pieces:
        steps = jax.random.uniform(jax.random.fold_in(jax.random.fold_in(key, 6), position), (parts,), jnp.float32, least / len(pieces), top_value / len(pieces))
        level = level * jnp.repeat(jnp.exp(steps), shape[position] // parts).reshape((-1,) + (1,) * (len(shape) - 1 - position))
    return level


def normal_values(stream_key, dims, scale, bound, shards=(), kind=jnp.bfloat16):
    values = jax.random.normal(stream_key, dims, jnp.float32) * scale
    if len(shards) > 0:
        values = levels(stream_key, dims, shards, -0.22, 0.18) * values
    return jnp.clip(values, min=-bound, max=bound).astype(kind)


def setup_inputs(seed: int = 0) -> dict:
    key_list = jax.random.split(jax.random.key(seed), 21)
    block_input = normal_values(key_list[0], (SEQS, LEN, D), 1.0, 6.0, ((0, 16), (1, 2)))
    cotangent = normal_values(key_list[1], (SEQS, LEN, D), 1.0, 6.0, ((0, 16), (1, 2)))
    attend = draw_attend(jax.random.fold_in(key_list[20], 71), 0)
    project = normal_values(key_list[3], (LAYERS, D, D), (D // 32) ** -0.5, 1.25, ((1, 8),), jnp.float32)
    expand = normal_values(key_list[4], (LAYERS, D, FF), D ** -0.5, 0.21875, ((1, 8),), jnp.float32)
    contract = normal_values(key_list[5], (LAYERS, FF, D), FF ** -0.5, 0.109375, ((1, 8),), jnp.float32)
    gains = jnp.clip(1.0 + 0.1 * jax.random.normal(key_list[6], (LAYERS, 2, D), jnp.float32), 0.5, 1.5)
    biases = normal_values(key_list[7], (LAYERS, 11, D), 0.2, 3.0, ((2, 8),), jnp.float32)
    attend_drift = normal_values(key_list[8], (LAYERS, D, 3 * D), (0.3 * (SEQS * LEN) ** 0.5), 112.0, ((1, 8),), jnp.float32)
    project_drift = normal_values(key_list[9], (LAYERS, D, D), (0.05 * (SEQS * LEN) ** 0.5), 20.0, ((1, 8),), jnp.float32)
    expand_drift = normal_values(key_list[10], (LAYERS, D, FF), (0.1 * (SEQS * LEN) ** 0.5), 40.0, ((1, 8),), jnp.float32)
    contract_drift = normal_values(key_list[11], (LAYERS, FF, D), (0.07 * (SEQS * LEN) ** 0.5), 28.0, ((1, 8),), jnp.float32)
    gains_drift = normal_values(key_list[12], (LAYERS, 2, D), (0.2 * (SEQS * LEN) ** 0.5), 80.0, ((2, 8),), jnp.float32)
    biases_drift = normal_values(key_list[13], (LAYERS, 11, D), (0.3 * (SEQS * LEN) ** 0.5), 112.0, ((2, 8),), jnp.float32)
    attend_spread = jnp.clip(jnp.exp(math.log(8192.0) - 3.6888794 * jax.random.uniform(key_list[14], (LAYERS, D, 3 * D), jnp.float32) ** levels(key_list[14], (LAYERS, D, 3 * D), ((1, 8),), -0.2, 0.2)), 204.8, 8192.0)
    project_spread = jnp.clip(jnp.exp(math.log(81.92) - 2.9957322 * jax.random.uniform(key_list[15], (LAYERS, D, D), jnp.float32) ** levels(key_list[15], (LAYERS, D, D), ((1, 8),), -0.2, 0.2)), 4.096, 81.92)
    expand_spread = jnp.clip(jnp.exp(math.log(409.6) - 2.9957323 * jax.random.uniform(key_list[16], (LAYERS, D, FF), jnp.float32) ** levels(key_list[16], (LAYERS, D, FF), ((1, 8),), -0.2, 0.2)), 20.48, 409.6)
    contract_spread = jnp.clip(jnp.exp(math.log(204.8) - 2.8134107 * jax.random.uniform(key_list[17], (LAYERS, FF, D), jnp.float32) ** levels(key_list[17], (LAYERS, FF, D), ((1, 8),), -0.2, 0.2)), 12.288, 204.8)
    gains_spread = jnp.clip(jnp.exp(math.log(1638.4) - 2.9957323 * jax.random.uniform(key_list[18], (LAYERS, 2, D), jnp.float32) ** levels(key_list[18], (LAYERS, 2, D), ((2, 8),), -0.2, 0.2)), 81.92, 1638.4)
    biases_spread = jnp.clip(jnp.exp(math.log(8192.0) - 3.6888794 * jax.random.uniform(key_list[19], (LAYERS, 11, D), jnp.float32) ** levels(key_list[19], (LAYERS, 11, D), ((2, 8),), -0.2, 0.2)), 204.8, 8192.0)
    return dict(block_input=block_input, cotangent=cotangent, attend=attend, project=project, expand=expand, contract=contract, gains=gains, biases=biases, attend_drift=attend_drift, project_drift=project_drift, expand_drift=expand_drift, contract_drift=contract_drift, gains_drift=gains_drift, biases_drift=biases_drift, attend_spread=attend_spread, project_spread=project_spread, expand_spread=expand_spread, contract_spread=contract_spread, gains_spread=gains_spread, biases_spread=biases_spread)


EPSILON = 1e-05
BETA_ONE = 0.9
BETA_TWO = 0.95
ADAM_FLOOR = 1e-08
RATE_MATRIX = 0.02
RATE_VECTOR = 0.1
DECAY = 0.01
NEGATIVE = -1e+30

def narrow_value(array):
    return array.astype(jnp.bfloat16)

def widen(array):
    return array.astype(jnp.float32)

def tables(positions):
    inverse = 10000.0 ** (-jnp.arange(0, ROT, 2, dtype=jnp.float32) / ROT)
    angles = positions.astype(jnp.float32)[:, None] * inverse[None, :]
    angles = jnp.concatenate([angles, angles], axis=1)
    return (jnp.cos(angles), jnp.sin(angles))

def split_heads(matrix):
    return matrix.reshape(matrix.shape[0], matrix.shape[1] // HEAD, HEAD)

def rotate(values, cosine, sine):
    half = ROT // 2
    front = values[..., :ROT]
    turned = jnp.concatenate([-front[..., half:], front[..., :half]], axis=-1)
    front = front * cosine[:, None, :] + turned * sine[:, None, :]
    return jnp.concatenate([front, values[..., ROT:]], axis=-1)

def rotate_back(grads, cosine, sine):
    half = ROT // 2
    front = grads[..., :ROT]
    sined = front * sine[:, None, :]
    backward_result = front * cosine[:, None, :] + jnp.concatenate([sined[..., half:], -sined[..., :half]], axis=-1)
    return jnp.concatenate([backward_result, grads[..., ROT:]], axis=-1)

def layer_norm_statistics(residual_stream):
    centred = residual_stream - lax.optimization_barrier(jnp.mean(residual_stream, axis=-1, keepdims=True))
    scale_factor = lax.rsqrt(lax.optimization_barrier(jnp.mean(centred * centred, axis=-1, keepdims=True)) + EPSILON)
    return (centred * scale_factor, scale_factor)

def layer_norm_backward(gradient_tree, normalized_input, scale_factor, gain_vector):
    reshaped_tensor = gradient_tree * gain_vector
    backward_result = (reshaped_tensor - lax.optimization_barrier(jnp.mean(reshaped_tensor, axis=-1, keepdims=True)) - normalized_input * lax.optimization_barrier(jnp.mean(reshaped_tensor * normalized_input, axis=-1, keepdims=True))) * scale_factor
    return (backward_result, lax.optimization_barrier(jnp.sum(gradient_tree * normalized_input, axis=0)), lax.optimization_barrier(jnp.sum(gradient_tree, axis=0)))

def gelu(inputs):
    return 0.5 * inputs * (1.0 + lax.erf(inputs * 0.7071067811865476))

def gelu_slope(inputs):
    return 0.5 * (1.0 + lax.erf(inputs * 0.7071067811865476)) + inputs * jnp.exp(-0.5 * inputs * inputs) * 0.3989422804014327

def attend_block(carry, query_tensor, positions, piece, start):
    maximum, total, accum = carry
    keys = split_heads(piece[0])
    values = split_heads(piece[1])
    count = keys.shape[0]
    scores = jnp.einsum('qhd,khd->hqk', widen(query_tensor), widen(keys)) * HEAD ** (-0.5)
    allowed = (positions[:, None] >= start + jnp.arange(count, dtype=jnp.int32)[None, :])[None]
    scores = jnp.where(allowed, scores, NEGATIVE)
    peak = jnp.maximum(maximum, lax.optimization_barrier(jnp.max(scores, axis=2)))
    shrink = jnp.exp(maximum - peak)
    weights = jnp.where(allowed, jnp.exp(scores - peak[:, :, None]), 0.0)
    total = total * shrink + lax.optimization_barrier(jnp.sum(weights, axis=2))
    accum = accum * jnp.transpose(shrink)[:, :, None] + jnp.einsum('hqk,khd->qhd', widen(narrow_value(weights)), widen(values))
    return (peak, total, accum)

def layer_forward(residual_stream, params, cosine, sine, positions):
    attend, project, expand, contract, gains, biases = params
    gain_float32 = widen(gains)
    bias_float32 = widen(biases)
    length, width = residual_stream.shape
    heads = width // HEAD
    normalized_input, scale_factor = layer_norm_statistics(residual_stream)
    first_normalized = narrow_value(normalized_input * gain_float32[0] + bias_float32[0])
    second_normalized = narrow_value(normalized_input * gain_float32[1] + bias_float32[1])
    mixed = jnp.dot(first_normalized, attend, preferred_element_type=jnp.float32) + bias_float32[4:7].reshape(-1)
    query_tensor = narrow_value(rotate(split_heads(mixed[:, :width]), cosine, sine))
    key_rows = narrow_value(rotate(split_heads(mixed[:, width:2 * width]), cosine, sine).reshape(length, width))
    value_rows = narrow_value(mixed[:, 2 * width:])
    start_carry = (jnp.full((heads, length), NEGATIVE, jnp.float32), jnp.zeros((heads, length), jnp.float32), jnp.zeros((length, heads, HEAD), jnp.float32))
    peak, total, accum = attend_block(start_carry, query_tensor, positions, (key_rows, value_rows), 0)
    context = accum / jnp.transpose(total)[:, :, None]
    log_sum_exp = peak + jnp.log(total)
    context_rows = narrow_value(context.reshape(length, width))
    attn_out = jnp.dot(context_rows, project, preferred_element_type=jnp.float32) + bias_float32[2]
    upper_bound = jnp.dot(second_normalized, expand, preferred_element_type=jnp.float32) + bias_float32[7:].reshape(-1)
    active_mask = narrow_value(gelu(upper_bound))
    branch = jnp.dot(active_mask, contract, preferred_element_type=jnp.float32) + bias_float32[3]
    saved_tensors = (normalized_input, scale_factor, first_normalized, second_normalized, query_tensor, key_rows, value_rows, context_rows, log_sum_exp, upper_bound, active_mask)
    return (residual_stream + attn_out + branch, saved_tensors)

def layer_backward(grad_out, params, saved_tensors, cosine, sine, positions):
    attend, project, expand, contract, gains, biases = params
    gain_float32 = widen(gains)
    normalized_input, scale_factor, first_normalized, second_normalized, query_tensor, key_rows, value_rows, context_rows, log_sum_exp, upper_bound, active_mask = saved_tensors
    length, width = grad_out.shape
    grad_b = narrow_value(grad_out)
    grad_contract = jnp.dot(active_mask.T, grad_b, preferred_element_type=jnp.float32)
    grad_project = jnp.dot(context_rows.T, grad_b, preferred_element_type=jnp.float32)
    grad_up = jnp.dot(grad_b, contract.T, preferred_element_type=jnp.float32) * gelu_slope(upper_bound)
    up_bias_gradient = narrow_value(grad_up)
    grad_context = split_heads(narrow_value(jnp.dot(grad_b, project.T, preferred_element_type=jnp.float32)))
    grad_expand = jnp.dot(second_normalized.T, up_bias_gradient, preferred_element_type=jnp.float32)
    second_backward, second_gain, second_shift = layer_norm_backward(jnp.dot(up_bias_gradient, expand.T, preferred_element_type=jnp.float32), normalized_input, scale_factor, gain_float32[1])
    keys = split_heads(key_rows)
    values = split_heads(value_rows)
    delta = lax.optimization_barrier(jnp.sum(widen(grad_context) * widen(split_heads(context_rows)), axis=-1)).T
    scores = jnp.einsum('qhd,khd->hqk', widen(query_tensor), widen(keys)) * HEAD ** (-0.5)
    allowed = (positions[:, None] >= positions[None, :])[None]
    scores = jnp.where(allowed, scores, NEGATIVE)
    probs = jnp.exp(scores - log_sum_exp[:, :, None])
    grad_probs = jnp.einsum('qhd,khd->hqk', widen(grad_context), widen(values))
    grad_scores = narrow_value(probs * (grad_probs - delta[:, :, None]) * HEAD ** (-0.5))
    grad_query = jnp.einsum('hqk,khd->qhd', widen(grad_scores), widen(keys))
    grad_key = jnp.einsum('hqk,qhd->khd', widen(grad_scores), widen(query_tensor))
    grad_value = jnp.einsum('hqk,qhd->khd', widen(narrow_value(probs)), widen(grad_context)).reshape(length, width)
    grad_mixed = jnp.concatenate([rotate_back(grad_query, cosine, sine).reshape(length, width), rotate_back(grad_key, cosine, sine).reshape(length, width), grad_value], axis=1)
    mixed_bias_gradient = narrow_value(grad_mixed)
    grad_attend = jnp.dot(first_normalized.T, mixed_bias_gradient, preferred_element_type=jnp.float32)
    first_backward, first_gain, first_shift = layer_norm_backward(jnp.dot(mixed_bias_gradient, attend.T, preferred_element_type=jnp.float32), normalized_input, scale_factor, gain_float32[0])
    grad_in = grad_out + first_backward + second_backward
    column = lax.optimization_barrier(jnp.sum(grad_out, axis=0))
    grad_gains = jnp.stack([first_gain, second_gain])
    grad_biases = jnp.concatenate([jnp.stack([first_shift, second_shift, column, column]), lax.optimization_barrier(jnp.sum(grad_mixed, axis=0)).reshape(3, width), lax.optimization_barrier(jnp.sum(grad_up, axis=0)).reshape(-1, width)], axis=0)
    return (grad_in, (grad_attend, grad_project, grad_expand, grad_contract, grad_gains, grad_biases))

def adam_step(weight, gradient_tree, drift, spread, rate):
    drift_new = BETA_ONE * drift + (1.0 - BETA_ONE) * gradient_tree
    spread_new = BETA_TWO * spread + (1.0 - BETA_TWO) * gradient_tree * gradient_tree
    mean_hat = drift_new / (1.0 - BETA_ONE ** STEP)
    square_hat = spread_new / (1.0 - BETA_TWO ** STEP)
    weight_new = weight - rate * (mean_hat / (jnp.sqrt(square_hat) + ADAM_FLOOR) + DECAY * weight)
    return (weight_new, drift_new, spread_new)

def reference(block_input, cotangent, attend, project, expand, contract, gains, biases, attend_drift, project_drift, expand_drift, contract_drift, gains_drift, biases_drift, attend_spread, project_spread, expand_spread, contract_spread, gains_spread, biases_spread):
    masters = (attend, project, expand, contract, gains, biases)
    params = [tuple((narrow_value(master[layer]) for master in masters)) for layer in range(LAYERS)]
    positions = jnp.arange(LEN, dtype=jnp.int32)
    cosine, sine = tables(positions)

    def one_sequence(totals, inputs):
        sequence, seq_grad = inputs
        residual_stream = widen(sequence)
        saved_all = []
        for layer in range(LAYERS):
            residual_stream, saved_tensors = layer_forward(residual_stream, params[layer], cosine, sine, positions)
            saved_all.append(saved_tensors)
        gradient_tree = widen(seq_grad)
        grads_all = [None] * LAYERS
        for layer in reversed(range(LAYERS)):
            gradient_tree, grads_all[layer] = layer_backward(gradient_tree, params[layer], saved_all[layer], cosine, sine, positions)
        stacked = tuple((jnp.stack([grads_all[layer][index] for layer in range(LAYERS)]) for index in range(6)))
        totals = tuple((total + part for total, part in zip(totals, stacked)))
        return (totals, (residual_stream, gradient_tree))
    start = tuple((jnp.zeros(master.shape, jnp.float32) for master in masters))
    totals, (outputs, input_grads) = lax.scan(one_sequence, start, (block_input, cotangent))
    drifts = (attend_drift, project_drift, expand_drift, contract_drift, gains_drift, biases_drift)
    spreads = (attend_spread, project_spread, expand_spread, contract_spread, gains_spread, biases_spread)
    rates = (RATE_MATRIX, RATE_MATRIX, RATE_MATRIX, RATE_MATRIX, RATE_VECTOR, RATE_VECTOR)
    updated = [adam_step(masters[index], totals[index], drifts[index], spreads[index], rates[index]) for index in range(6)]
    return (outputs, input_grads, totals[0], totals[1], totals[2], totals[3], totals[4], totals[5], updated[0][0], updated[1][0], updated[2][0], updated[3][0], updated[4][0], updated[5][0], updated[0][1], updated[1][1], updated[2][1], updated[3][1], updated[4][1], updated[5][1], updated[0][2], updated[1][2], updated[2][2], updated[3][2], updated[4][2], updated[5][2])
```

```python
import functools

import jax
import jax.numpy as jnp
from jax import lax
from jax.experimental import pallas as pl
from jax.experimental.pallas import tpu as pltpu
from jax.sharding import PartitionSpec as P

HEAD = 64
ROT = 16
STEP = 3


EPSILON = 1e-05
BETA_ONE = 0.9
BETA_TWO = 0.95
ADAM_FLOOR = 1e-08
RATE_MATRIX = 0.02
RATE_VECTOR = 0.1
DECAY = 0.01
NEGATIVE = -1e30


def narrow_value(array):
    return array.astype(jnp.bfloat16)


def tables(positions):
    inverse = 10000.0 ** (-jnp.arange(0, ROT, 2, dtype=jnp.float32) / ROT)
    angles = positions.astype(jnp.float32)[:, None] * inverse[None, :]
    angles = jnp.concatenate([angles, angles], axis=1)
    return (jnp.cos(angles), jnp.sin(angles))


def split_heads(matrix):
    return matrix.reshape(matrix.shape[0], matrix.shape[1] // HEAD, HEAD)


def rotate(values, cosine, sine):
    half = ROT // 2
    front = values[..., :ROT]
    turned = jnp.concatenate([-front[..., half:], front[..., :half]], axis=-1)
    front = front * cosine[:, None, :] + turned * sine[:, None, :]
    return jnp.concatenate([front, values[..., ROT:]], axis=-1)


def rotate_back(grads, cosine, sine):
    half = ROT // 2
    front = grads[..., :ROT]
    sined = front * sine[:, None, :]
    backward_result = front * cosine[:, None, :] + jnp.concatenate(
        [sined[..., half:], -sined[..., :half]], axis=-1
    )
    return jnp.concatenate([backward_result, grads[..., ROT:]], axis=-1)


def layer_norm_statistics(residual_stream):
    centred = residual_stream - jnp.mean(residual_stream, axis=-1, keepdims=True)
    scale_factor = lax.rsqrt(jnp.mean(centred * centred, axis=-1, keepdims=True) + EPSILON)
    return (centred * scale_factor, scale_factor)


def layer_norm_backward(gradient_tree, normalized_input, scale_factor, gain_vector):
    reshaped_tensor = gradient_tree * gain_vector
    backward_result = (
        reshaped_tensor
        - jnp.mean(reshaped_tensor, axis=-1, keepdims=True)
        - normalized_input * jnp.mean(reshaped_tensor * normalized_input, axis=-1, keepdims=True)
    ) * scale_factor
    return (
        backward_result,
        jnp.sum(gradient_tree * normalized_input, axis=0),
        jnp.sum(gradient_tree, axis=0),
    )


def gelu(inputs):
    return 0.5 * inputs * (1.0 + lax.erf(inputs * 0.7071067811865476))


def gelu_slope(inputs):
    return (
        0.5 * (1.0 + lax.erf(inputs * 0.7071067811865476))
        + inputs * jnp.exp(-0.5 * inputs * inputs) * 0.3989422804014327
    )


def attend_block(carry, query_tensor, positions, piece):
    maximum, total, accum = carry
    keys = split_heads(piece[0])
    values = split_heads(piece[1])
    count = keys.shape[0]
    scores = jnp.einsum(
        "qhd,khd->hqk", query_tensor, keys, preferred_element_type=jnp.float32
    ) * HEAD ** (-0.5)
    allowed = (positions[:, None] >= jnp.arange(count, dtype=jnp.int32)[None, :])[None]
    scores = jnp.where(allowed, scores, NEGATIVE)
    peak = jnp.maximum(maximum, jnp.max(scores, axis=2))
    weights = jnp.where(allowed, jnp.exp(scores - peak[:, :, None]), 0.0)
    total = jnp.sum(weights, axis=2)
    accum = jnp.einsum(
        "hqk,khd->qhd", narrow_value(weights), values, preferred_element_type=jnp.float32
    )
    return (peak, total, accum)


def fetch_weights(shards):
    return (
        lax.all_gather(shards[0], ("shard", "ctx"), axis=0, tiled=True),
        lax.all_gather(shards[1], ("shard", "ctx"), axis=0, tiled=True),
        lax.all_gather(shards[2], ("shard", "ctx"), axis=0, tiled=True),
        lax.all_gather(shards[3], ("shard", "ctx"), axis=0, tiled=True),
        lax.all_gather(shards[4], ("shard", "ctx"), axis=1, tiled=True),
        lax.all_gather(shards[5], ("shard", "ctx"), axis=1, tiled=True),
    )


def sum_grads(local):
    owned = (
        lax.psum_scatter(local[0], ("shard", "ctx"), scatter_dimension=0, tiled=True),
        lax.psum_scatter(local[1], ("shard", "ctx"), scatter_dimension=0, tiled=True),
        lax.psum_scatter(local[2], ("shard", "ctx"), scatter_dimension=0, tiled=True),
        lax.psum_scatter(local[3], ("shard", "ctx"), scatter_dimension=0, tiled=True),
        lax.psum_scatter(local[4], ("shard", "ctx"), scatter_dimension=1, tiled=True),
        lax.psum_scatter(local[5], ("shard", "ctx"), scatter_dimension=1, tiled=True),
    )
    return lax.psum((owned[0], owned[1], owned[2], owned[3], owned[4], owned[5]), "rep")


def layer_forward(residual_stream, params, cosine, sine, positions):
    attend, project, expand, contract, gains, biases = params
    gain_float32 = gains.astype(jnp.float32)
    bias_float32 = biases.astype(jnp.float32)
    span, width = residual_stream.shape
    heads = width // HEAD
    normalized_input, scale_factor = layer_norm_statistics(residual_stream)
    first_normalized = narrow_value(normalized_input * gain_float32[0] + bias_float32[0])
    second_normalized = narrow_value(normalized_input * gain_float32[1] + bias_float32[1])
    mixed = jnp.dot(first_normalized, attend, preferred_element_type=jnp.float32) + bias_float32[
        4:7
    ].reshape(-1)
    query_tensor = narrow_value(rotate(split_heads(mixed[:, :width]), cosine, sine))
    key_rows = narrow_value(
        rotate(split_heads(mixed[:, width : 2 * width]), cosine, sine).reshape(span, width)
    )
    value_rows = narrow_value(mixed[:, 2 * width :])
    start_carry = (
        jnp.full((heads, span), NEGATIVE, jnp.float32),
        jnp.zeros((heads, span), jnp.float32),
        jnp.zeros((span, heads, HEAD), jnp.float32),
    )
    peak, total, accum = attend_block(
        start_carry,
        query_tensor,
        positions,
        (
            lax.all_gather(key_rows, "ctx", axis=0, tiled=True),
            lax.all_gather(value_rows, "ctx", axis=0, tiled=True),
        ),
    )
    context = accum / jnp.transpose(total)[:, :, None]
    log_sum_exp = peak + jnp.log(total)
    context_rows = narrow_value(context.reshape(span, width))
    attn_out = jnp.dot(context_rows, project, preferred_element_type=jnp.float32) + bias_float32[2]
    upper_bound = jnp.dot(
        second_normalized, expand, preferred_element_type=jnp.float32
    ) + bias_float32[7:].reshape(-1)
    active_mask = narrow_value(gelu(upper_bound))
    branch = jnp.dot(active_mask, contract, preferred_element_type=jnp.float32) + bias_float32[3]
    saved_tensors = (
        normalized_input,
        scale_factor,
        first_normalized,
        second_normalized,
        query_tensor,
        key_rows,
        value_rows,
        context_rows,
        log_sum_exp,
        upper_bound,
        active_mask,
        None,
    )
    return (residual_stream + attn_out + branch, saved_tensors)


def layer_backward(grad_out, params, saved_tensors, cosine, sine, positions):
    attend, project, expand, contract, gains, biases = params
    gain_float32 = gains.astype(jnp.float32)
    (
        normalized_input,
        scale_factor,
        first_normalized,
        second_normalized,
        query_tensor,
        key_rows,
        value_rows,
        context_rows,
        log_sum_exp,
        upper_bound,
        active_mask,
        full_keys,
    ) = saved_tensors
    span, width = grad_out.shape
    grad_b = narrow_value(grad_out)
    grad_contract = jnp.dot(active_mask.T, grad_b, preferred_element_type=jnp.float32)
    grad_project = jnp.dot(context_rows.T, grad_b, preferred_element_type=jnp.float32)
    grad_up = jnp.dot(grad_b, contract.T, preferred_element_type=jnp.float32) * gelu_slope(
        upper_bound
    )
    up_bias_gradient = narrow_value(grad_up)
    grad_context = split_heads(
        narrow_value(jnp.dot(grad_b, project.T, preferred_element_type=jnp.float32))
    )
    grad_expand = jnp.dot(second_normalized.T, up_bias_gradient, preferred_element_type=jnp.float32)
    second_backward, second_gain, second_shift = layer_norm_backward(
        jnp.dot(up_bias_gradient, expand.T, preferred_element_type=jnp.float32),
        normalized_input,
        scale_factor,
        gain_float32[1],
    )
    keys_all, values_all = (
        lax.all_gather(key_rows, "ctx", axis=0, tiled=True),
        lax.all_gather(value_rows, "ctx", axis=0, tiled=True),
    )
    length = keys_all.shape[0]
    keys = split_heads(keys_all)
    values = split_heads(values_all)
    delta = jnp.einsum(
        "qhd,qhd->hq", grad_context, split_heads(context_rows), preferred_element_type=jnp.float32
    )
    scores = jnp.einsum(
        "qhd,khd->hqk", query_tensor, keys, preferred_element_type=jnp.float32
    ) * HEAD ** (-0.5)
    allowed = (positions[:, None] >= jnp.arange(length, dtype=jnp.int32)[None, :])[None]
    probs = jnp.where(
        allowed, jnp.exp(jnp.where(allowed, scores, NEGATIVE) - log_sum_exp[:, :, None]), 0.0
    )
    grad_probs = jnp.einsum(
        "qhd,khd->hqk", grad_context, values, preferred_element_type=jnp.float32
    )
    grad_scores = narrow_value(probs * (grad_probs - delta[:, :, None]) * HEAD ** (-0.5))
    grad_query = jnp.einsum("hqk,khd->qhd", grad_scores, keys, preferred_element_type=jnp.float32)
    key_terms = jnp.einsum(
        "hqk,qhd->khd", grad_scores, query_tensor, preferred_element_type=jnp.float32
    ).reshape(length, width)
    value_terms = jnp.einsum(
        "hqk,qhd->khd", narrow_value(probs), grad_context, preferred_element_type=jnp.float32
    ).reshape(length, width)
    grad_key, grad_value = (
        lax.psum_scatter(key_terms, "ctx", scatter_dimension=0, tiled=True),
        lax.psum_scatter(value_terms, "ctx", scatter_dimension=0, tiled=True),
    )
    grad_mixed = jnp.concatenate(
        [
            rotate_back(grad_query, cosine, sine).reshape(span, width),
            rotate_back(split_heads(grad_key), cosine, sine).reshape(span, width),
            grad_value,
        ],
        axis=1,
    )
    mixed_bias_gradient = narrow_value(grad_mixed)
    grad_attend = jnp.dot(
        first_normalized.T, mixed_bias_gradient, preferred_element_type=jnp.float32
    )
    first_backward, first_gain, first_shift = layer_norm_backward(
        jnp.dot(mixed_bias_gradient, attend.T, preferred_element_type=jnp.float32),
        normalized_input,
        scale_factor,
        gain_float32[0],
    )
    grad_in = grad_out + first_backward + second_backward
    column = jnp.sum(grad_out, axis=0)
    grad_gains = jnp.stack([first_gain, second_gain])
    grad_biases = jnp.concatenate(
        [
            jnp.stack([first_shift, second_shift, column, column]),
            jnp.sum(grad_mixed, axis=0).reshape(3, width),
            jnp.sum(grad_up, axis=0).reshape(-1, width),
        ],
        axis=0,
    )
    return (
        grad_in,
        (grad_attend, grad_project, grad_expand, grad_contract, grad_gains, grad_biases),
    )


def adam_step(weight, gradient_tree, drift, spread, rate):
    drift_new = BETA_ONE * drift + (1.0 - BETA_ONE) * gradient_tree
    spread_new = BETA_TWO * spread + (1.0 - BETA_TWO) * gradient_tree * gradient_tree
    mean_hat = drift_new / (1.0 - BETA_ONE**STEP)
    square_hat = spread_new / (1.0 - BETA_TWO**STEP)
    weight_new = weight - rate * (mean_hat / (jnp.sqrt(square_hat) + ADAM_FLOOR) + DECAY * weight)
    return (weight_new, drift_new, spread_new)


def general_body(
    block_input,
    cotangent,
    attend,
    project,
    expand,
    contract,
    gains,
    biases,
    attend_drift,
    project_drift,
    expand_drift,
    contract_drift,
    gains_drift,
    biases_drift,
    attend_spread,
    project_spread,
    expand_spread,
    contract_spread,
    gains_spread,
    biases_spread,
):
    span = block_input.shape[1]
    layers = attend.shape[0]
    positions = lax.axis_index("ctx") * span + jnp.arange(span, dtype=jnp.int32)
    cosine, sine = tables(positions)
    masters = (attend, project, expand, contract, gains, biases)
    residual_stream = block_input[0].astype(jnp.float32)
    params_all = []
    saved_all = []
    for layer in range(layers):
        params = fetch_weights(tuple((narrow_value(master[layer]) for master in masters)))
        residual_stream, saved_tensors = layer_forward(
            residual_stream, params, cosine, sine, positions
        )
        params_all.append(params)
        saved_all.append(saved_tensors)
    gradient_tree = cotangent[0].astype(jnp.float32)
    grads_all = [None] * layers
    for layer in reversed(range(layers)):
        gradient_tree, local = layer_backward(
            gradient_tree, params_all[layer], saved_all[layer], cosine, sine, positions
        )
        grads_all[layer] = sum_grads(local)
    totals = tuple(
        (jnp.stack([grads_all[layer][index] for layer in range(layers)]) for index in range(6))
    )
    drifts = (attend_drift, project_drift, expand_drift, contract_drift, gains_drift, biases_drift)
    spreads = (
        attend_spread,
        project_spread,
        expand_spread,
        contract_spread,
        gains_spread,
        biases_spread,
    )
    rates = (RATE_MATRIX, RATE_MATRIX, RATE_MATRIX, RATE_MATRIX, RATE_VECTOR, RATE_VECTOR)
    updated = [
        adam_step(masters[index], totals[index], drifts[index], spreads[index], rates[index])
        for index in range(6)
    ]
    return (
        residual_stream[None],
        gradient_tree[None],
        totals[0],
        totals[1],
        totals[2],
        totals[3],
        totals[4],
        totals[5],
        updated[0][0],
        updated[1][0],
        updated[2][0],
        updated[3][0],
        updated[4][0],
        updated[5][0],
        updated[0][1],
        updated[1][1],
        updated[2][1],
        updated[3][1],
        updated[4][1],
        updated[5][1],
        updated[0][2],
        updated[1][2],
        updated[2][2],
        updated[3][2],
        updated[4][2],
        updated[5][2],
    )


def wide(values):
    return values.astype(jnp.float32)


def mat(left, right):
    return jnp.dot(left, right, preferred_element_type=jnp.float32)


def mat_tokens(left, right):
    return lax.dot_general(
        left, right, (((0,), (0,)), ((), ())), preferred_element_type=jnp.float32
    )


def mat_back(left, right):
    return lax.dot_general(
        left, right, (((1,), (1,)), ((), ())), preferred_element_type=jnp.float32
    )


def turn_terms(values, tables_ref):
    half, lanes = ROT // 2, values.shape[1]
    return pltpu.roll(values, lanes - half, 1) * tables_ref[1] + pltpu.roll(
        values, half, 1
    ) * tables_ref[2]


def causal_mask(length, span, part):
    query = lax.broadcasted_iota(jnp.int32, (length, length), 0) + part * span
    key = lax.broadcasted_iota(jnp.int32, (length, length), 1) + part * span
    query = jnp.where(query >= length, query - length, query)
    key = jnp.where(key >= length, key - length, key)
    return query >= key


def head_weights(query, key, allowed):
    scores = jnp.where(allowed, mat_back(query, key) * HEAD ** (-0.5), NEGATIVE)
    raw = jnp.exp(scores - jnp.max(scores, axis=1, keepdims=True))
    raw = jnp.where(allowed, raw, 0.0)
    return raw, jnp.sum(raw, axis=1, keepdims=True)


def attend_kernel(
    span, flags, x_ref, attend_ref, project_ref, small_ref, bias_ref, tables_ref, qkv_ref, context_ref, out_ref
):
    length, head_width = context_ref.shape[1:]
    turned = 2 * head_width
    first = narrow_value(wide(x_ref[0]) * small_ref[0:1] + small_ref[2:3])
    mixed = mat(first, attend_ref[...]) + bias_ref[...]
    pairs = mixed[:, :turned]
    pairs = narrow_value(pairs * tables_ref[0] + turn_terms(pairs, tables_ref))
    value_rows = narrow_value(mixed[:, turned:])
    qkv_ref[0, :, :turned] = pairs
    qkv_ref[0, :, turned:] = value_rows
    allowed = causal_mask(length, span, flags[1])
    for start in range(0, head_width, HEAD):
        query = pairs[:, start : start + HEAD]
        key = pairs[:, head_width + start : head_width + start + HEAD]
        raw, total = head_weights(query, key, allowed)
        context = mat(narrow_value(raw), value_rows[:, start : start + HEAD]) / total
        context_ref[0, :, start : start + HEAD] = narrow_value(context)
    out_ref[0] = mat(context_ref[0], project_ref[...])


def hidden_kernel(
    flags, x_ref, expand_ref, contract_ref, small_ref, bias_ref, attn_ref, kept_ref, sent_ref
):
    step = pl.program_id(0)
    second = narrow_value(wide(x_ref[0]) * small_ref[1:2] + small_ref[3:4])
    upper = mat(second, expand_ref[...]) + bias_ref[...]
    total = mat(narrow_value(gelu(upper)), contract_ref[...])
    total = total + jnp.where(step // 2 == flags[0] // 2, attn_ref[0], 0.0)

    @pl.when(step % 2 == 0)
    def _():
        kept_ref[0] = total

    @pl.when(step % 2 == 1)
    def _():
        sent_ref[0] = narrow_value(total)


def attend_back_kernel(
    span,
    flags,
    x_ref,
    grad_ref,
    qkv_ref,
    context_ref,
    attend_ref,
    project_ref,
    small_ref,
    tables_ref,
    kept_ref,
    sent_ref,
    project_kept_ref,
    project_sent_ref,
    shifted_ref,
    sums_ref,
    mixed_sums_ref,
    attend_sum,
    project_sum,
    mixed_rows,
):
    step = pl.program_id(0)
    length, head_width = context_ref.shape[1:]
    turned = 2 * head_width

    @pl.when(step == 0)
    def _():
        attend_sum[...] = jnp.zeros_like(attend_sum)
        project_sum[...] = jnp.zeros_like(project_sum)
        sums_ref[...] = jnp.zeros_like(sums_ref)
        mixed_sums_ref[...] = jnp.zeros_like(mixed_sums_ref)

    grad = grad_ref[0]
    context = context_ref[0]
    grad_context = narrow_value(mat_back(grad, project_ref[...]))
    project_sum[...] += mat_tokens(context, grad)
    allowed = causal_mask(length, span, flags[1])
    products = wide(grad_context) * wide(context)
    for start in range(0, head_width, HEAD):
        query = qkv_ref[0, :, start : start + HEAD]
        key = qkv_ref[0, :, head_width + start : head_width + start + HEAD]
        value = qkv_ref[0, :, turned + start : turned + start + HEAD]
        slope = grad_context[:, start : start + HEAD]
        delta = jnp.sum(products[:, start : start + HEAD], axis=1, keepdims=True)
        raw, total = head_weights(query, key, allowed)
        probs = raw / total
        grad_scores = narrow_value(probs * (mat_back(slope, value) - delta) * HEAD ** (-0.5))
        mixed_rows[:, start : start + HEAD] = mat(grad_scores, key)
        mixed_rows[:, head_width + start : head_width + start + HEAD] = mat_tokens(
            grad_scores, query
        )
        mixed_rows[:, turned + start : turned + start + HEAD] = mat_tokens(
            narrow_value(probs), slope
        )
    pairs = mixed_rows[:, :turned]
    mixed_rows[:, :turned] = pairs * tables_ref[0] - turn_terms(pairs, tables_ref)
    grad_mixed = mixed_rows[...]
    mixed_sums_ref[0:1] += jnp.sum(grad_mixed, axis=0, keepdims=True)
    grad_mixed = narrow_value(grad_mixed)
    x = wide(x_ref[0])
    first = narrow_value(x * small_ref[0:1] + small_ref[2:3])
    attend_sum[...] += mat_tokens(first, grad_mixed)
    grad_first = mat_back(grad_mixed, attend_ref[...])
    sums_ref[0:1] += jnp.sum(grad_first * x, axis=0, keepdims=True)
    sums_ref[1:2] += jnp.sum(grad_first, axis=0, keepdims=True)
    shifted_ref[0] = grad_first * small_ref[0:1]

    @pl.when(step == pl.num_programs(0) - 1)
    def _():
        shards, rows = kept_ref.shape[:2]
        for index in range(shards):
            kept_ref[index] = attend_sum[pl.ds((2 * index + flags[1]) * rows, rows), :]
            sent_ref[index] = narrow_value(
                attend_sum[pl.ds((2 * index + 1 - flags[1]) * rows, rows), :]
            )
        project_kept_ref[...] = project_sum[pl.ds(flags[1] * rows, rows), :]
        project_sent_ref[...] = narrow_value(project_sum[pl.ds((1 - flags[1]) * rows, rows), :])


def hidden_back_kernel(joined, flags, x_ref, grad_ref, expand_ref, contract_ref, small_ref, bias_ref, *refs):
    first_ref, refs = (refs[0], refs[1:]) if joined else (None, refs)
    up_kept_ref, up_sent_ref, down_kept_ref, down_sent_ref, kept_ref, sent_ref = refs[:6]
    sums_ref, upper_sums_ref, contract_sum, expand_sum = refs[6:]
    step = pl.program_id(0)

    @pl.when(step == 0)
    def _():
        contract_sum[...] = jnp.zeros_like(contract_sum)
        expand_sum[...] = jnp.zeros_like(expand_sum)
        sums_ref[...] = jnp.zeros_like(sums_ref)
        upper_sums_ref[...] = jnp.zeros_like(upper_sums_ref)

    grad = grad_ref[0]
    x = wide(x_ref[0])
    second = narrow_value(x * small_ref[1:2] + small_ref[3:4])
    upper = mat(second, expand_ref[...]) + bias_ref[...]
    contract_sum[...] += mat_tokens(narrow_value(gelu(upper)), grad)
    grad_up = mat_back(grad, contract_ref[...]) * gelu_slope(upper)
    upper_sums_ref[0:1] += jnp.sum(grad_up, axis=0, keepdims=True)
    up_rows = narrow_value(grad_up)
    expand_sum[...] += mat_tokens(second, up_rows)
    grad_second = mat_back(up_rows, expand_ref[...])
    sums_ref[0:1] += jnp.sum(grad_second * x, axis=0, keepdims=True)
    sums_ref[1:2] += jnp.sum(grad_second, axis=0, keepdims=True)
    total = grad_second * small_ref[1:2]
    if joined:
        total = total + jnp.where(step // 2 == flags[0] // 2, first_ref[0], 0.0)

    @pl.when(step % 2 == 0)
    def _():
        kept_ref[0] = total

    @pl.when(step % 2 == 1)
    def _():
        sent_ref[0] = narrow_value(total)

    @pl.when(step == pl.num_programs(0) - 1)
    def _():
        halves, rows, _ = down_kept_ref.shape
        slice_width = expand_sum.shape[1]
        for index in range(halves):
            for up_ref, down_ref, near in (
                (up_kept_ref, down_kept_ref, flags[2]),
                (up_sent_ref, down_sent_ref, 1 - flags[2]),
            ):
                place = 2 * index + near
                down_ref[index] = narrow_value(contract_sum[pl.ds(place * rows, rows), :])
                for part in range(2):
                    begin = part * slice_width
                    up_ref[index, :, begin : begin + slice_width] = narrow_value(
                        expand_sum[pl.ds((2 * place + part) * rows, rows), :]
                    )


def fold_kernel(kept_ref, got_ref, own_ref, east_ref, north_ref, corner_ref):
    span = own_ref.shape[0]
    total = kept_ref[...] + wide(got_ref[...])
    own_ref[...] = total[0, :span]
    north_ref[...] = narrow_value(total[0, span:])
    east_ref[...] = narrow_value(total[1, :span])
    corner_ref[...] = narrow_value(total[1, span:])


def join(own_ref, east_ref, north_ref, corner_ref):
    return own_ref[...] + wide(east_ref[...]) + wide(north_ref[...]) + wide(corner_ref[...])


def stream_kernel(
    own_ref, east_ref, north_ref, corner_ref, stream_ref, bias_ref, out_ref, norm_ref, scale_ref, sent_ref
):
    stream = stream_ref[...] + join(own_ref, east_ref, north_ref, corner_ref) + bias_ref[...]
    out_ref[...] = stream
    normalized, scale = layer_norm_statistics(stream)
    norm_ref[...] = normalized
    scale_ref[...] = scale
    sent_ref[...] = narrow_value(normalized)


def output_kernel(own_ref, east_ref, north_ref, corner_ref, stream_ref, bias_ref, out_ref):
    out_ref[...] = (
        stream_ref[...] + join(own_ref, east_ref, north_ref, corner_ref) + bias_ref[...]
    )


def gradient_kernel(
    own_ref, east_ref, north_ref, corner_ref, grad_ref, norm_ref, scale_ref, out_ref, sent_ref
):
    shifted = join(own_ref, east_ref, north_ref, corner_ref)
    normalized = norm_ref[...]
    grad = grad_ref[...] + scale_ref[...] * (
        shifted
        - jnp.mean(shifted, axis=-1, keepdims=True)
        - normalized * jnp.mean(shifted * normalized, axis=-1, keepdims=True)
    )
    out_ref[...] = grad
    sent_ref[...] = narrow_value(grad)


def call_plain(kernel, inputs, outputs):
    elements = sum(array.size for array in inputs)
    return pl.pallas_call(
        kernel,
        out_shape=[jax.ShapeDtypeStruct(shape, dtype) for shape, dtype in outputs],
        cost_estimate=pl.CostEstimate(
            flops=8 * elements, bytes_accessed=6 * elements, transcendentals=0
        ),
    )(*inputs)


def whole(shape):
    return pl.BlockSpec(shape, lambda step, flags: (0,) * len(shape))


def call_kernel(kernel, grid, inputs, outputs, scratch, flags, flops, transcendentals=0):
    moved = sum(array.size * array.dtype.itemsize for array, _ in inputs)
    for shape, dtype, _ in outputs:
        size = jnp.dtype(dtype).itemsize
        for extent in shape:
            size *= extent
        moved += size
    return pl.pallas_call(
        kernel,
        out_shape=[jax.ShapeDtypeStruct(shape, dtype) for shape, dtype, _ in outputs],
        grid_spec=pltpu.PrefetchScalarGridSpec(
            num_scalar_prefetch=1,
            grid=(grid,),
            in_specs=[spec for _, spec in inputs],
            out_specs=[spec for _, _, spec in outputs],
            scratch_shapes=scratch,
        ),
        compiler_params=pltpu.CompilerParams(dimension_semantics=("arbitrary",)),
        cost_estimate=pl.CostEstimate(
            flops=flops, bytes_accessed=moved, transcendentals=transcendentals
        ),
    )(flags, *[array for array, _ in inputs])


def store_update(gradient, weight_ref, drift_ref, spread_ref, outputs, rate):
    outputs[0][0] = gradient
    updated = adam_step(weight_ref[0], gradient, drift_ref[0], spread_ref[0], rate)
    for target, value in zip(outputs[1:], updated):
        target[0] = value


def late_update_kernel(aliased, late_ref, *refs):
    inputs, outputs = refs[:3], refs[3 + aliased :]
    reps, _, mixed_width = late_ref.shape
    head_width = mixed_width // 3
    gradient = jnp.concatenate(
        [
            wide(late_ref[index, :, third * head_width : (third + 1) * head_width])
            for third in range(3)
            for index in range(reps)
        ],
        axis=1,
    )
    store_update(gradient, *inputs, outputs, RATE_MATRIX)


def up_update_kernel(piece, aliased, expand_ref, project_ref, *refs):
    inputs, outputs = refs[:6], refs[6 + aliased :]
    reps, _, columns = expand_ref.shape
    shards = columns // 2 // piece
    gradient = jnp.concatenate(
        [
            wide(expand_ref[index, :, (part * shards + place) * piece :][:, :piece])
            for place in range(shards)
            for part in range(2)
            for index in range(reps)
        ],
        axis=1,
    )
    store_update(gradient, *inputs[:3], outputs[:4], RATE_MATRIX)
    gradient = wide(project_ref[0])
    for index in range(1, reps):
        gradient = gradient + wide(project_ref[index])
    store_update(gradient, *inputs[3:], outputs[4:], RATE_MATRIX)


def down_update_kernel(aliased, contract_ref, *refs):
    gradient = wide(contract_ref[...]).reshape(-1, contract_ref.shape[2])
    store_update(gradient, *refs[:3], refs[3 + aliased :], RATE_MATRIX)


def update_layer(kernel, steps, layer, sums, params, previous):
    specs, outs = [], []
    for weight, _, _ in params:
        _, height, columns = weight.shape
        spec = pl.BlockSpec((1, height // steps, columns), lambda step: (layer, step, 0))
        specs += [spec] * 3
        outs += [(jax.ShapeDtypeStruct(weight.shape, jnp.float32), spec)] * 4
    operands = [array for array, _ in sums] + [array for param in params for array in param]
    in_specs = [spec for _, spec in sums] + specs
    aliases = {}
    if previous is not None:
        aliases = {len(operands) + index: index for index in range(len(previous))}
        operands += list(previous)
        in_specs += [pl.BlockSpec(memory_space=pl.ANY)] * len(previous)
    count = sum(param[0].size for param in params) // params[0][0].shape[0]
    return pl.pallas_call(
        functools.partial(kernel, len(aliases)),
        out_shape=[shape for shape, _ in outs],
        grid=(steps,),
        in_specs=in_specs,
        out_specs=[spec for _, spec in outs],
        input_output_aliases=aliases,
        compiler_params=pltpu.CompilerParams(dimension_semantics=("arbitrary",)),
        cost_estimate=pl.CostEstimate(
            flops=16 * count, bytes_accessed=30 * count, transcendentals=count
        ),
    )(*operands)


def after(values, *tokens):
    return lax.optimization_barrier((values, tokens))[0]


def flip_pairs(sizes, flips):
    total = 1
    for size in sizes:
        total *= size
    pairs = []
    for source in range(total):
        rest, coords = source, []
        for size in reversed(sizes):
            coords.append(rest % size)
            rest //= size
        coords.reverse()
        target = 0
        for size, coord, flip in zip(sizes, coords, flips):
            target = target * size + (coord ^ flip)
        pairs.append((source, target))
    return pairs


def grouped_body(mesh_shape, *arrays):
    block_input, cotangent, attend, project, expand, contract, gains, biases = arrays[:8]
    drifts, spreads = arrays[8:14], arrays[14:20]
    masters = arrays[2:8]
    reps, shards, parts = mesh_shape["rep"], mesh_shape["shard"], mesh_shape["ctx"]
    rep, shard, ctx = lax.axis_index("rep"), lax.axis_index("shard"), lax.axis_index("ctx")
    outer, inner = rep // 2, rep % 2
    layers, rows, _ = attend.shape
    span, width = block_input.shape[1:]
    length = span * parts
    tokens = length * reps
    hidden = expand.shape[2]
    owned_seqs = reps // parts
    owned_tokens = owned_seqs * length
    head_width = width // reps
    mixed_width = 3 * head_width
    heads = head_width // HEAD
    block = contract.shape[1]
    piece = block // reps
    slice_width = piece * shards
    group = ("rep", "ctx")
    sizes = (2, 2, parts)
    to_outer = flip_pairs(sizes, (1, 0, 0))
    to_part = flip_pairs(sizes, (0, 0, 1))
    to_corner = flip_pairs(sizes, (1, 0, 1))
    transpose = [(a * shards + b, b * shards + a) for a in range(reps) for b in range(shards)]

    def swap_part(values):
        return lax.ppermute(values, "ctx", flip_pairs((2,), (1,)))

    def swap_inner(values):
        return lax.ppermute(values, "rep", flip_pairs((2, 2), (0, 1)))

    def swap_outer(values):
        return lax.ppermute(values, "rep", flip_pairs((2, 2), (1, 0)))

    def swap_near(values):
        return lax.ppermute(values, "shard", flip_pairs((2, 2), (0, 1)))

    def swap_far(values):
        return lax.ppermute(values, "shard", flip_pairs((2, 2), (1, 0)))

    def swap_mirror(values):
        return lax.ppermute(values, "shard", flip_pairs((2, 2), (1, 1)))

    def pair(index, own, other, axis=0):
        first = jnp.where(index == 0, own, other)
        second = jnp.where(index == 0, other, own)
        return jnp.stack([first, second], axis=axis)

    def gather_shard(values, first_token=None, second_token=None):
        mirror = swap_mirror(values if first_token is None else after(values, first_token))
        if second_token is not None:
            mirror = after(mirror, second_token)
        near = swap_near(jnp.stack([values, mirror]))
        same = pair(shard % 2, values, near[0])
        other = pair(shard % 2, near[1], mirror)
        return pair(shard // 2, same, other).reshape((shards,) + values.shape), mirror

    def gather_rep(values):
        across = pair(outer, values, swap_outer(values))
        return pair(inner, across, swap_inner(across), axis=1).reshape((reps,) + values.shape)

    def gather_tokens(values):
        east = lax.ppermute(values, group, to_outer)
        north = lax.ppermute(values, group, to_part)
        corner = lax.ppermute(values, group, to_corner)
        plane = jnp.stack([values, north, east, corner]).reshape(2, parts, span, -1)
        other = swap_inner(plane)
        return jnp.stack([plane, other], axis=1).reshape(reps, length, -1)

    def scatter_start(kept, sent):
        row = (span, width)
        own, east, north, corner = call_plain(
            fold_kernel,
            [kept, swap_inner(sent)],
            [(row, jnp.float32), (row, jnp.bfloat16), (row, jnp.bfloat16), (row, jnp.bfloat16)],
        )
        return own, east, north, corner

    def scatter_end(own, east, north, corner):
        corner = lax.ppermute(corner, group, to_corner)
        east = lax.ppermute(east, group, to_outer)
        north = lax.ppermute(north, group, to_part)
        return own, east, north, corner

    chosen = outer ^ ctx

    flags = jnp.stack([chosen * owned_seqs, ctx, shard % 2]).astype(jnp.int32)

    def head_columns(matrix):
        return jnp.concatenate(
            [
                lax.dynamic_slice_in_dim(matrix, third * width + rep * head_width, head_width, 1)
                for third in range(3)
            ],
            axis=1,
        )

    def hidden_columns(matrix, part):
        return jnp.concatenate(
            [
                lax.dynamic_slice_in_dim(
                    matrix, (index * parts + part) * block + rep * piece, piece, 1
                )
                for index in range(shards)
            ],
            axis=1,
        )

    small_rows = jnp.concatenate([gains, biases], axis=1)
    small_count = small_rows.shape[1]
    small_rows = jnp.transpose(narrow_value(small_rows).reshape(layers * small_count, rows))
    expand_own = [narrow_value(hidden_columns(expand[n], ctx)) for n in range(layers)]
    expand_sent = [narrow_value(hidden_columns(expand[n], 1 - ctx)) for n in range(layers)]
    expand_got = swap_part(jnp.concatenate(expand_sent, axis=1)).reshape(rows, layers, slice_width)
    project_part = lax.ppermute(narrow_value(project), ("rep", "shard"), transpose)
    project_full = pair(ctx, project_part, swap_part(project_part), axis=1).reshape(
        layers, head_width, width
    )

    def attend_piece(n):
        return narrow_value(head_columns(attend[n]))

    def hidden_piece(n):
        both = pair(ctx, expand_own[n], expand_got[:, n]).reshape(parts, rows, slice_width)
        rows_down = narrow_value(lax.dynamic_slice_in_dim(contract[n], rep * piece, piece, 0))
        return jnp.concatenate([both[0], both[1], rows_down], axis=1)

    def attend_matrix(gathered):
        full = pair(ctx, gathered, swap_part(gathered), axis=1)
        return full.reshape(width, -1)

    def hidden_matrices(gathered):
        up = gathered[..., : parts * slice_width].reshape(shards, rows, parts, slice_width)
        up = jnp.transpose(up, (0, 2, 1, 3)).reshape(width, slice_width)
        return up, gathered[..., parts * slice_width :].reshape(slice_width, width)

    lead_piece = jnp.concatenate([attend_piece(0), small_rows], axis=1)
    lead, lead_token = gather_shard(lead_piece)
    lead = attend_matrix(lead)
    small_full = wide(jnp.transpose(lead[:, mixed_width:])).reshape(layers, small_count, width)
    hidden_all, _ = gather_shard(hidden_piece(0), lead_token)
    weights = [(lead[:, :mixed_width], project_full[0]) + hidden_matrices(hidden_all)]

    def fetch_rest(n, first_token, second_token):
        everything = jnp.concatenate([hidden_piece(n), attend_piece(n)], axis=1)
        everything, _ = gather_shard(everything, first_token, second_token)
        edge = parts * slice_width + width
        attend_full = attend_matrix(everything[..., edge:])
        return (attend_full, project_full[n]) + hidden_matrices(everything[..., :edge])

    positions = jnp.concatenate(
        [(ctx ^ part) * span + jnp.arange(span, dtype=jnp.int32) for part in range(parts)]
    )
    cosine, sine = tables(positions)
    half = ROT // 2
    still = HEAD - ROT
    turning = jnp.stack(
        [
            jnp.pad(cosine, ((0, 0), (0, still)), constant_values=1.0),
            jnp.pad(-sine[:, :half], ((0, 0), (0, HEAD - half))),
            jnp.pad(sine[:, half:], ((0, 0), (half, still))),
        ]
    )
    turning = jnp.tile(turning, (1, 1, 2 * heads))

    def own_rows(lane):
        return pl.BlockSpec((1, length, width), lambda step, flags: (flags[0] + step, 0, lane))

    def step_rows(lane):
        return pl.BlockSpec((1, length, width), lambda step, flags: (step, 0, lane))

    half_rows = pl.BlockSpec((1, length, width), lambda step, flags: (step // 2, 0, 0))
    inner_rows = pl.BlockSpec((1, length, width), lambda step, flags: (step % 2, 0, 0))

    def steps(columns):
        return pl.BlockSpec((1, length, columns), lambda step, flags: (step, 0, 0))

    halves = (owned_seqs, length, width)

    def hidden_bias(small):
        return lax.dynamic_slice_in_dim(small[9:], (ctx * reps + rep) * piece, piece, 1).reshape(1, -1)

    def attend_forward(gathered, weights, small):
        attend_full, project_full, _, _ = weights
        mixed_bias = lax.dynamic_slice_in_dim(small[6:9], rep * head_width, head_width, 1)
        return call_kernel(
            functools.partial(attend_kernel, span),
            owned_seqs,
            [
                (gathered[0], own_rows(gathered[1])),
                (attend_full, whole(attend_full.shape)),
                (project_full, whole(project_full.shape)),
                (small, whole(small.shape)),
                (mixed_bias.reshape(1, -1), whole((1, mixed_width))),
                (turning, whole(turning.shape)),
            ],
            [
                ((owned_seqs, length, mixed_width), jnp.bfloat16, steps(mixed_width)),
                ((owned_seqs, length, head_width), jnp.bfloat16, steps(head_width)),
                (halves, jnp.float32, step_rows(0)),
            ],
            [],
            flags,
            2 * owned_tokens * (width * (mixed_width + head_width) + 2 * length * head_width),
            owned_tokens * length * heads,
        )

    def hidden_forward(gathered, attn, weights, small):
        _, _, expand_full, contract_full = weights
        bias = hidden_bias(small)
        return call_kernel(
            hidden_kernel,
            reps,
            [
                (gathered[0], step_rows(gathered[1])),
                (expand_full, whole(expand_full.shape)),
                (contract_full, whole(contract_full.shape)),
                (small, whole(small.shape)),
                (bias, whole(bias.shape)),
                (attn, inner_rows),
            ],
            [(halves, jnp.float32, half_rows), (halves, jnp.bfloat16, half_rows)],
            [],
            flags,
            4 * tokens * width * slice_width,
            tokens * slice_width,
        )

    def attend_backward(grad_rows, gathered, qkv, context, weights, small):
        attend_full, project_full, _, _ = weights
        return call_kernel(
            functools.partial(attend_back_kernel, span),
            owned_seqs,
            [
                (gathered[0], own_rows(gathered[1])),
                (grad_rows[0], own_rows(grad_rows[1])),
                (qkv, steps(mixed_width)),
                (context, steps(head_width)),
                (attend_full, whole(attend_full.shape)),
                (project_full, whole(project_full.shape)),
                (small, whole(small.shape)),
                (turning, whole(turning.shape)),
            ],
            [
                ((shards, rows, mixed_width), jnp.float32, whole((shards, rows, mixed_width))),
                ((shards, rows, mixed_width), jnp.bfloat16, whole((shards, rows, mixed_width))),
                ((rows, width), jnp.float32, whole((rows, width))),
                ((rows, width), jnp.bfloat16, whole((rows, width))),
                (halves, jnp.float32, step_rows(0)),
                ((8, width), jnp.float32, whole((8, width))),
                ((8, mixed_width), jnp.float32, whole((8, mixed_width))),
            ],
            [
                pltpu.VMEM((width, mixed_width), jnp.float32),
                pltpu.VMEM((head_width, width), jnp.float32),
                pltpu.VMEM((length, mixed_width), jnp.float32),
            ],
            flags,
            4 * owned_tokens * width * (mixed_width + head_width)
            + 10 * owned_tokens * length * head_width,
            owned_tokens * length * heads,
        )

    def hidden_backward(grad_rows, gathered, first_shifted, weights, small):
        _, _, expand_full, contract_full = weights
        bias = hidden_bias(small)
        joined = first_shifted is not None
        up = (owned_seqs, rows, parts * slice_width)
        down = (owned_seqs, rows, width)
        return call_kernel(
            functools.partial(hidden_back_kernel, joined),
            reps,
            [
                (gathered[0], step_rows(gathered[1])),
                (grad_rows[0], step_rows(grad_rows[1])),
                (expand_full, whole(expand_full.shape)),
                (contract_full, whole(contract_full.shape)),
                (small, whole(small.shape)),
                (bias, whole(bias.shape)),
            ]
            + ([(first_shifted, inner_rows)] if joined else []),
            [
                (up, jnp.bfloat16, whole(up)),
                (up, jnp.bfloat16, whole(up)),
                (down, jnp.bfloat16, whole(down)),
                (down, jnp.bfloat16, whole(down)),
                (halves, jnp.float32, half_rows),
                (halves, jnp.bfloat16, half_rows),
                ((8, width), jnp.float32, whole((8, width))),
                ((8, slice_width), jnp.float32, whole((8, slice_width))),
            ],
            [
                pltpu.VMEM((slice_width, width), jnp.float32),
                pltpu.VMEM((width, slice_width), jnp.float32),
            ],
            flags,
            10 * tokens * width * slice_width,
            2 * tokens * slice_width,
        )

    def small_gradient(grad_out, first_sums, mixed_sums, second_sums, upper_sums):
        column = jnp.sum(grad_out, axis=0, keepdims=True)
        lanes = jnp.arange(width)[None, :]
        mixed_rows = jnp.tile(mixed_sums[0].reshape(3, head_width), (1, reps))
        mixed_rows = jnp.where(lanes // head_width == rep, mixed_rows, 0.0)
        upper_rows = jnp.tile(upper_sums[0].reshape(shards, piece), (1, width // piece))
        upper_rows = jnp.where(lanes // piece == ctx * reps + rep, upper_rows, 0.0)
        return jnp.concatenate(
            [
                first_sums[0:1],
                second_sums[0:1],
                first_sums[1:2],
                second_sums[1:2],
                column,
                column,
                mixed_rows,
                upper_rows,
            ]
        )

    def fold_part(blocks, axis):
        kept = lax.dynamic_index_in_dim(blocks, ctx, axis, keepdims=False)
        sent = lax.dynamic_index_in_dim(blocks, 1 - ctx, axis, keepdims=False)
        return kept, sent

    def far_half(total):
        kept = lax.dynamic_index_in_dim(total, shard // 2, 0, keepdims=False)
        sent = lax.dynamic_index_in_dim(total, 1 - shard // 2, 0, keepdims=False)
        return kept, narrow_value(sent)

    def near_half(blocks):
        blocks = blocks.reshape((2, 2) + blocks.shape[1:])
        kept = lax.dynamic_index_in_dim(blocks, shard % 2, 1, keepdims=False)
        sent = lax.dynamic_index_in_dim(blocks, 1 - shard % 2, 1, keepdims=False)
        return kept, narrow_value(sent)

    def update_up(layer, early, previous):
        edge = parts * slice_width
        steps_up = 2
        sums = [
            (early, pl.BlockSpec((reps, rows // steps_up, edge), lambda step: (0, step, 0))),
            (
                early,
                pl.BlockSpec((reps, rows // steps_up, width), lambda step: (0, step, edge // width)),
            ),
        ]
        params = [(masters[index], drifts[index], spreads[index]) for index in (2, 1)]
        kernel = functools.partial(up_update_kernel, piece)
        return update_layer(kernel, steps_up, layer, sums, params, previous)

    def update_down(layer, early, previous):
        steps_down = 2
        spec = pl.BlockSpec((reps // steps_down, rows, width), lambda step: (step, 0, 0))
        params = [(masters[3], drifts[3], spreads[3])]
        return update_layer(
            down_update_kernel, steps_down, layer, [(early, spec)], params, previous
        )

    def update_late(layer, late, previous):
        steps_late = 2
        spec = pl.BlockSpec((reps, rows // steps_late, mixed_width), lambda step: (0, step, 0))
        params = [(masters[0], drifts[0], spreads[0])]
        return update_layer(late_update_kernel, steps_late, layer, [(late, spec)], params, previous)

    def reduce_small(values):
        for swap in (swap_part, swap_near, swap_far, swap_inner, swap_outer):
            values = values + swap(values)
        values = lax.dynamic_slice_in_dim(values, (shard * parts + ctx) * rows, rows, 1)
        return values.reshape(layers, small_count, rows)

    def fold_far(kept, got):
        kept, sent = far_half(wide(kept) + wide(got))
        return kept, swap_far(sent)

    def finish_project(kept, got):
        return lax.ppermute(narrow_value(kept + wide(got)), ("rep", "shard"), transpose)

    def finish_up(kept, got, project_sum):
        up = narrow_value(kept + wide(got)).reshape(rows, parts, slice_width)
        kept, sent = fold_part(up, 1)
        up = pair(ctx, kept, swap_part(sent), axis=1).reshape(rows, -1)
        return gather_rep(jnp.concatenate([up, project_sum], axis=1))

    def finish_plain(kept, got):
        return gather_rep(narrow_value(kept + wide(got)))

    def attend_near(kept, got):
        kept, sent = near_half(kept + wide(got))
        return kept, swap_near(sent)

    row = (span, width)
    stream = wide(block_input[0])
    grad_last = wide(cotangent[0])
    normalized, scale = layer_norm_statistics(stream)
    first_statistics = (normalized, scale)
    tokens_sent = after(
        jnp.concatenate([narrow_value(normalized), cotangent[0]], axis=1), lead_piece
    )
    both = gather_tokens(tokens_sent)
    first_tokens, last_rows = (both, 0), (both, 1)
    qkv_first, context_first, attn = attend_forward(first_tokens, weights[0], small_full[0])
    weights.append(fetch_rest(1, hidden_all, attn))
    kept, sent = hidden_forward(first_tokens, attn, weights[0], small_full[0])
    bias = (small_full[0][4] + small_full[0][5]).reshape(1, width)
    stream, normalized, scale, sent = call_plain(
        stream_kernel,
        [*scatter_end(*scatter_start(kept, sent)), stream, bias],
        [(row, jnp.float32), (row, jnp.float32), ((span, 1), jnp.float32), (row, jnp.bfloat16)],
    )
    last_tokens = (gather_tokens(sent), 0)
    small = small_full[1]
    qkv, context, attn = attend_forward(last_tokens, weights[1], small)
    (
        attend_kept,
        attend_sent,
        project_kept,
        project_sent,
        first_shifted,
        first_sums,
        mixed_sums,
    ) = attend_backward(last_rows, last_tokens, qkv, context, weights[1], small)
    attend_got = swap_part(attend_sent)
    project_got = swap_part(project_sent)
    up_kept, up_sent, down_kept, down_sent, kept, sent, second_sums, upper_sums = hidden_backward(
        last_rows, last_tokens, first_shifted, weights[1], small
    )
    scattered = scatter_start(kept, sent)
    up_got = swap_near(after(up_sent, scattered[1]))
    down_got = swap_near(after(down_sent, scattered[1]))
    scattered = scatter_end(*scattered)
    hidden_tokens, attn = after((last_tokens[0], attn), up_sent, scattered[0])
    out_kept, out_sent = hidden_forward((hidden_tokens, 0), attn, weights[1], small)
    grad, grad_sent = call_plain(
        gradient_kernel,
        [*scattered, grad_last, normalized, scale],
        [(row, jnp.float32), (row, jnp.bfloat16)],
    )
    small_last = small_gradient(grad_last, first_sums, mixed_sums, second_sums, upper_sums)
    first_rows = (gather_tokens(grad_sent), 0)
    attend_kept, attend_got, up_kept, up_got = after(
        (attend_kept, attend_got, up_kept, up_got), grad_sent
    )
    attend_kept, attend_got = attend_near(attend_kept, attend_got)
    up_kept, up_got = fold_far(up_kept, up_got)
    small = small_full[0]
    (
        up_kept_first,
        up_sent,
        down_kept_first,
        down_sent,
        kept,
        sent,
        second_sums,
        upper_sums,
    ) = hidden_backward(first_rows, first_tokens, None, weights[0], small)
    down_kept, down_got, attend_kept, attend_got, project_kept, project_got = after(
        (down_kept, down_got, attend_kept, attend_got, project_kept, project_got), up_sent
    )
    down_kept, down_got = fold_far(down_kept, down_got)
    attend_kept, attend_got = fold_far(attend_kept, attend_got)
    project_sum = finish_project(project_kept, project_got)
    up_got_first = swap_near(up_sent)
    down_got_first = swap_near(down_sent)
    (
        attend_kept_first,
        attend_sent,
        project_kept,
        project_sent,
        first_shifted,
        first_sums,
        mixed_sums,
    ) = attend_backward(first_rows, first_tokens, qkv_first, context_first, weights[0], small)
    attend_got_first = swap_part(attend_sent)
    project_got = swap_part(project_sent)
    small_first = small_gradient(grad, first_sums, mixed_sums, second_sums, upper_sums)
    up_kept, up_got, project_sum, down_kept, down_got, attend_kept, attend_got = after(
        (up_kept, up_got, project_sum, down_kept, down_got, attend_kept, attend_got), first_shifted
    )
    up_all = update_up(1, finish_up(up_kept, up_got, project_sum), None)
    down_all = update_down(1, finish_plain(down_kept, down_got), None)
    late_all = update_late(1, finish_plain(attend_kept, attend_got), None)
    up_kept, up_got = fold_far(up_kept_first, up_got_first)
    down_kept, down_got = fold_far(down_kept_first, down_got_first)
    attend_kept, attend_got = attend_near(attend_kept_first, attend_got_first)
    project_sum = finish_project(project_kept, project_got)
    attend_kept, attend_got = fold_far(attend_kept, attend_got)
    up_all = update_up(0, finish_up(up_kept, up_got, project_sum), up_all)
    down_all = update_down(0, finish_plain(down_kept, down_got), down_all)
    late_all = update_late(0, finish_plain(attend_kept, attend_got), late_all)
    chosen_rows = (jnp.arange(owned_seqs) == chosen)[:, None, None]
    kept = kept + jnp.where(chosen_rows, first_shifted[0][None], 0.0)
    sent = narrow_value(wide(sent) + jnp.where(chosen_rows, first_shifted[1][None], 0.0))
    grad, _ = call_plain(
        gradient_kernel,
        [*scatter_end(*scatter_start(kept, sent)), grad, *first_statistics],
        [(row, jnp.float32), (row, jnp.bfloat16)],
    )
    bias = (small_full[1][4] + small_full[1][5]).reshape(1, width)
    out_sent = after(out_sent, first_rows[0])
    (stream,) = call_plain(
        output_kernel,
        [*scatter_end(*scatter_start(out_kept, out_sent)), stream, bias],
        [(row, jnp.float32)],
    )
    small_total = reduce_small(jnp.concatenate([small_first, small_last]))
    totals = (small_total[:, :2], small_total[:, 2:])
    updated = [
        adam_step(masters[4 + index], totals[index], drifts[4 + index], spreads[4 + index], RATE_VECTOR)
        for index in range(2)
    ]
    kinds = []
    for kind in range(4):
        kinds += [late_all[kind], up_all[4 + kind], up_all[kind], down_all[kind]]
        kinds += list(totals) if kind == 0 else [update[kind - 1] for update in updated]
    return (stream[None], grad[None]) + tuple(kinds)


def body(mesh_shape, *arrays):
    pairs = mesh_shape["rep"] == 4 and mesh_shape["shard"] == 4 and mesh_shape["ctx"] == 2
    if pairs and arrays[2].shape[0] == 2:
        return grouped_body(mesh_shape, *arrays)
    return general_body(*arrays)


def solution(mesh):
    in_specs = (
        P(("rep", "shard"), "ctx", None),
        P(("rep", "shard"), "ctx", None),
        P(None, ("shard", "ctx"), None),
        P(None, ("shard", "ctx"), None),
        P(None, ("shard", "ctx"), None),
        P(None, ("shard", "ctx"), None),
        P(None, None, ("shard", "ctx")),
        P(None, None, ("shard", "ctx")),
        P(None, ("shard", "ctx"), None),
        P(None, ("shard", "ctx"), None),
        P(None, ("shard", "ctx"), None),
        P(None, ("shard", "ctx"), None),
        P(None, None, ("shard", "ctx")),
        P(None, None, ("shard", "ctx")),
        P(None, ("shard", "ctx"), None),
        P(None, ("shard", "ctx"), None),
        P(None, ("shard", "ctx"), None),
        P(None, ("shard", "ctx"), None),
        P(None, None, ("shard", "ctx")),
        P(None, None, ("shard", "ctx")),
    )
    out_specs = (
        P(("rep", "shard"), "ctx", None),
        P(("rep", "shard"), "ctx", None),
        P(None, ("shard", "ctx"), None),
        P(None, ("shard", "ctx"), None),
        P(None, ("shard", "ctx"), None),
        P(None, ("shard", "ctx"), None),
        P(None, None, ("shard", "ctx")),
        P(None, None, ("shard", "ctx")),
        P(None, ("shard", "ctx"), None),
        P(None, ("shard", "ctx"), None),
        P(None, ("shard", "ctx"), None),
        P(None, ("shard", "ctx"), None),
        P(None, None, ("shard", "ctx")),
        P(None, None, ("shard", "ctx")),
        P(None, ("shard", "ctx"), None),
        P(None, ("shard", "ctx"), None),
        P(None, ("shard", "ctx"), None),
        P(None, ("shard", "ctx"), None),
        P(None, None, ("shard", "ctx")),
        P(None, None, ("shard", "ctx")),
        P(None, ("shard", "ctx"), None),
        P(None, ("shard", "ctx"), None),
        P(None, ("shard", "ctx"), None),
        P(None, ("shard", "ctx"), None),
        P(None, None, ("shard", "ctx")),
        P(None, None, ("shard", "ctx")),
    )
    return jax.shard_map(functools.partial(body, dict(mesh.shape)), mesh=mesh, in_specs=in_specs, out_specs=out_specs, check_vma=False)
```
